256 devices in a mesh: outer: 8 (over y, core), inner: 32 (over x, z).
Axes of the slice: x: 4, y: 4, z: 8, core: 2. Of those that a mesh axis runs over, the one named last changes fastest.
Arguments:
- query_states: bfloat16 [65536, 4096], P(('outer', 'inner')), may hold values from -486 to 486
- key_states: bfloat16 [65536, 4096], P(('outer', 'inner')), may hold values from -18 to 18
- value_states: bfloat16 [65536, 4096], P(('outer', 'inner')), may hold values from -6 to 6
- doc_lengths: int32 [128], replicated, may hold values from 1 to 768, 65536 in all
Outputs:
- attended: bfloat16 [65536, 4096], P(('outer', 'inner'))
The draws below stay inside these ranges and needn't reach their ends.
Inputs may be any that keep to these rules, and one draw needn't show every extreme that they name: `doc_lengths`: 128 document lengths summing to 65536; the longest is exactly 768.
All inputs are finite; a program needn't handle non-finite values.
Results may differ from the reference program's by a relative error of at most 0.0045.
Values may be sent and summed in bfloat16 or wider, within the bound.
A program may use at most 192 MiB of HBM per device.

```python
import math
import jax
import jax.numpy as jnp
import numpy as np
from jax import lax

HEADS = 32
HEAD_DIM = 128
TOK_DEV = 256
SPAN = 3
TOKENS = 65536
MAXDOC = 768
NDOCS = 128


def shared_bases(key):
    row_count = TOKENS
    col_count = HEADS * HEAD_DIM
    base_keys = jnp.clip(jax.random.normal(jax.random.fold_in(key, 11), (row_count, col_count), jnp.float32), -4.5, 4.5)
    base_queries = jnp.clip(jax.random.normal(jax.random.fold_in(key, 12), (row_count, col_count), jnp.float32), -4.5, 4.5)
    return (base_keys, base_queries)


def draw_key_states(key, part):
    base_keys, base_queries = shared_bases(key)
    result = base_keys
    return result.astype(jnp.bfloat16)


def draw_query_states(key, part):
    base_keys, base_queries = shared_bases(key)
    result = base_queries
    return result.astype(jnp.bfloat16)


def shard_levels(stream_key, dims, shards, smallest, high):
    def one(axis_at, blocks):
        heights = jax.random.uniform(jax.random.fold_in(jax.random.fold_in(stream_key, 6), axis_at), (blocks,), jnp.float32, smallest / len(shards), high / len(shards))
        return jnp.repeat(jnp.exp(heights), dims[axis_at] // blocks).reshape((-1,) + (1,) * (len(dims) - axis_at - 1))

    level = one(*shards[0])
    for cut in shards[1:]:
        level = level * one(*cut)
    return level


def profile(amount, total, bound, lean):
    portions = [(1 << 20) // math.isqrt(rank ** lean) + 1 for rank in range(2, amount + 1)]
    surplus, given = total - bound - (amount - 1), [1] * (amount - 1)
    while surplus > 0:
        candidates = [i for i in range(amount - 1) if given[i] < bound]
        pool, budget = sum([portions[i] for i in candidates]), surplus
        for i in candidates:
            more = min(bound - given[i], max(1, budget * portions[i] // pool), surplus)
            given[i] = given[i] + more
            surplus = surplus - more
    return np.array([bound] + given)


def uneven_parts(rng, number_of, total, most, skew):
    if number_of == 2:
        one = jax.random.randint(rng, (), max(1, total - most), min(most, total - 1) + 1)
        return jnp.stack([one, total - one])
    sizes = jnp.asarray(profile(number_of, total, most, skew), jnp.int32)
    twos = (number_of - 1) // 2
    source_of, sink = sizes[1:1 + 2 * twos:2], sizes[2:2 + 2 * twos:2]
    slack = jnp.minimum(source_of - 1, most - sink)
    moved = jax.random.randint(jax.random.fold_in(rng, 1), (twos,), 0, 1 << 20) % (slack + 1)
    sizes = sizes.at[1:1 + 2 * twos:2].set(source_of - moved).at[2:2 + 2 * twos:2].set(sink + moved)
    return sizes[jax.random.permutation(jax.random.fold_in(rng, 2), number_of)]


def noise(own_key, dims, width, limit, shards=(), kind=jnp.bfloat16):
    factor_of = shard_levels(own_key, dims, shards, -0.22, 0.18) if shards else 1.0
    values = jax.random.normal(own_key, dims, jnp.float32) * width * factor_of
    return jnp.minimum(jnp.maximum(values, -limit), limit).astype(kind)


def setup_inputs(seed: int = 0) -> dict:
    key_list = jax.random.split(jax.random.key(seed), 5)
    return {
        "query_states": draw_query_states(jax.random.fold_in(key_list[4], 71), 0),
        "key_states": draw_key_states(jax.random.fold_in(key_list[4], 71), 0),
        "value_states": noise(key_list[2], (TOKENS, HEADS * HEAD_DIM), 1.0, 6.0, ((0, 256),)),
        "doc_lengths": uneven_parts(key_list[3], NDOCS, TOKENS, MAXDOC, 2).astype(jnp.int32),
    }


def doc_numbers(doc_lengths, positions):
    doc_ends = jnp.cumsum(doc_lengths).astype(jnp.int32)
    inside = (positions >= 0) & (positions < TOKENS)
    counted = lax.optimization_barrier(jnp.sum((doc_ends[None, :] <= positions[:, None]).astype(jnp.int32), axis=1)).astype(jnp.int32)
    return jnp.where(inside, counted, -1).astype(jnp.int32)

def reference(query_states, key_states, value_states, doc_lengths):
    margin = SPAN * TOK_DEV
    window = (2 * SPAN + 1) * TOK_DEV
    scaling = 1.0 / math.sqrt(HEAD_DIM)
    padded_keys = jnp.pad(key_states, ((margin, margin), (0, 0)))
    padded_values = jnp.pad(value_states, ((margin, margin), (0, 0)))
    positions = jnp.arange(TOKENS + 2 * margin, dtype=jnp.int32) - margin
    padded_docs = doc_numbers(doc_lengths, positions)

    def one_block(block_index):
        first_row = (block_index * TOK_DEV).astype(jnp.int32)
        query_block = lax.dynamic_slice_in_dim(query_states, first_row, TOK_DEV, 0).astype(jnp.float32).reshape(TOK_DEV, HEADS, HEAD_DIM)
        key_block = lax.dynamic_slice_in_dim(padded_keys, first_row, window, 0).astype(jnp.float32).reshape(window, HEADS, HEAD_DIM)
        value_block = lax.dynamic_slice_in_dim(padded_values, first_row, window, 0).astype(jnp.float32).reshape(window, HEADS, HEAD_DIM)
        query_docs = lax.dynamic_slice_in_dim(padded_docs, first_row + margin, TOK_DEV, 0)
        key_docs = lax.dynamic_slice_in_dim(padded_docs, first_row, window, 0)
        same_doc = (query_docs[:, None] == key_docs[None, :])[None]
        scores = jnp.einsum('qhd,khd->hqk', query_block, key_block) * scaling
        masked = jnp.where(same_doc, scores, -jnp.inf)
        row_peak = lax.optimization_barrier(jnp.max(masked, axis=2, keepdims=True))
        weights = jnp.where(same_doc, jnp.exp(masked - row_peak), 0.0)
        totals = lax.optimization_barrier(jnp.sum(weights, axis=2))
        rounded = lax.optimization_barrier(weights.astype(jnp.bfloat16)).astype(jnp.float32)
        summed = jnp.einsum('hqk,khd->qhd', rounded, value_block)
        result = summed / jnp.transpose(totals)[:, :, None]
        return result.astype(jnp.bfloat16).reshape(TOK_DEV, HEADS * HEAD_DIM)
    blocks_out = lax.map(one_block, jnp.arange(TOKENS // TOK_DEV, dtype=jnp.int32))
    return blocks_out.reshape(TOKENS, HEADS * HEAD_DIM)
```

```python
import functools
import math

import jax
import jax.numpy as jnp
from jax import lax
from jax.experimental import pallas as pl
from jax.experimental.pallas import tpu as pltpu
from jax.sharding import PartitionSpec as P

HEADS = 32
SPAN = 3
RING = 8
MESH = pl.DeviceIdType.MESH
MASKED = -1e30


def kernel(
    outer_size,
    inner_size,
    lengths_ref,
    query_ref,
    key_ref,
    value_ref,
    out_ref,
    keys,
    values,
    queries,
    results,
    doc_rows,
    doc_cols,
    key_send,
    key_recv,
    value_send,
    value_recv,
    query_send,
    query_recv,
    result_send,
    result_recv,
    halo_send,
    halo_recv,
    own_sem,
):
    rows = query_ref.shape[0]
    size = keys.shape[2]
    own_heads = keys.shape[0]
    group_cols = own_heads * size
    halo_rows = SPAN * rows
    doc_total = lengths_ref.shape[0]
    blocks = outer_size * inner_size
    outer = lax.axis_index("outer")
    inner = lax.axis_index("inner")
    place = lax.rem(inner, RING)
    line_start = inner - place
    block_index = outer * inner_size + inner

    def ring_device(other):
        return (outer, line_start + other)

    def group_device(step):
        other = lax.rem(block_index + step * RING + blocks, blocks)
        return (lax.div(other, inner_size), lax.rem(other, inner_size))

    def ring_place(offset):
        return lax.rem(place + offset, RING)

    def columns(owner, head):
        return pl.ds(pl.multiple_of(owner * group_cols + head * size, size), size)

    def key_slot(head, source):
        return keys.at[head, pl.ds(pl.multiple_of(halo_rows + source * rows, rows), rows), :]

    def value_slot(head, source):
        return values.at[head, pl.ds(pl.multiple_of(halo_rows + source * rows, rows), rows), :]

    def query_slot(head, source):
        return queries.at[head, pl.ds(pl.multiple_of(source * rows, rows), rows), :]

    def result_slot(head, target):
        return results.at[head, pl.ds(pl.multiple_of(target * rows, rows), rows), :]

    streams = {
        "key": (key_ref, key_slot, key_send, key_recv),
        "value": (value_ref, value_slot, value_send, value_recv),
        "query": (query_ref, query_slot, query_send, query_recv),
    }

    def ring_copy(kind, head, offset):
        source, slot, send, recv = streams[kind]
        owner = ring_place(offset)
        return pltpu.make_async_remote_copy(
            src_ref=source.at[:, columns(owner, head)],
            dst_ref=slot(head, place),
            send_sem=send.at[head, owner],
            recv_sem=recv.at[head, place],
            device_id=ring_device(owner),
            device_id_type=MESH,
        )

    def ring_arrival(kind, head, offset):
        source, slot, send, recv = streams[kind]
        other = ring_place(offset)
        return pltpu.make_async_remote_copy(
            src_ref=source.at[:, columns(other, head)],
            dst_ref=slot(head, other),
            send_sem=send.at[head, other],
            recv_sem=recv.at[head, other],
            device_id=ring_device(other),
            device_id_type=MESH,
        )

    def own_copy(kind, head):
        source, slot, send, recv = streams[kind]
        return pltpu.make_async_copy(
            source.at[:, columns(place, head)], slot(head, place), recv.at[head, place]
        )

    def halo_copy(which, head, up):
        buffer = (keys, values)[which]
        edge = halo_rows + RING * rows
        source_row = edge - halo_rows if up else halo_rows
        target_row = 0 if up else edge
        return pltpu.make_async_remote_copy(
            src_ref=buffer.at[head, pl.ds(source_row, halo_rows), :],
            dst_ref=buffer.at[head, pl.ds(target_row, halo_rows), :],
            send_sem=halo_send.at[head, which, 0 if up else 1],
            recv_sem=halo_recv.at[head, which, 0 if up else 1],
            device_id=group_device(1 if up else -1),
            device_id_type=MESH,
        )

    def result_copy(head, target):
        return pltpu.make_async_remote_copy(
            src_ref=result_slot(head, target),
            dst_ref=out_ref.at[:, columns(place, head)],
            send_sem=result_send.at[head, target],
            recv_sem=result_recv.at[head, place],
            device_id=ring_device(target),
            device_id_type=MESH,
        )

    def result_arrival(head, source):
        return pltpu.make_async_remote_copy(
            src_ref=result_slot(head, source),
            dst_ref=out_ref.at[:, columns(source, head)],
            send_sem=result_send.at[head, source],
            recv_sem=result_recv.at[head, source],
            device_id=ring_device(source),
            device_id_type=MESH,
        )

    barrier = pltpu.get_barrier_semaphore()
    for offset in range(1, RING):
        pl.semaphore_signal(
            barrier, inc=1, device_id=ring_device(ring_place(offset)), device_id_type=MESH
        )
    for step in (1, -1):
        pl.semaphore_signal(
            barrier, inc=1, device_id=group_device(step), device_id_type=MESH
        )
    pl.semaphore_wait(barrier, RING + 1)

    order = (1, 7, 2, 6, 3, 5, 4)

    @pl.loop(0, own_heads)
    def _(head):
        for kind in ("key", "value", "query"):
            own_copy(kind, head).start()
            for offset in order:
                ring_copy(kind, head, offset).start()

    window = 2 * SPAN + RING
    first_position = (block_index - place - SPAN) * rows
    positions = (
        first_position
        + lax.broadcasted_iota(jnp.int32, doc_rows.shape, 0) * rows
        + lax.broadcasted_iota(jnp.int32, doc_rows.shape, 1)
    )

    def count(doc, carry):
        end, counted = carry
        end = end + lengths_ref[doc]
        return end, counted + jnp.where(positions >= end, 1, 0)

    _, counted = lax.fori_loop(0, doc_total, count, (jnp.int32(0), jnp.zeros_like(positions)))
    inside = (positions >= 0) & (positions < blocks * rows)
    doc_rows[...] = jnp.where(inside, counted, -1).astype(jnp.float32)
    for block in range(RING):
        row = doc_rows[SPAN + block : SPAN + block + 1, :]
        doc_cols[block * rows : (block + 1) * rows, :] = jnp.transpose(
            jnp.broadcast_to(row, (rows, rows))
        )

    scaling = 1.0 / math.sqrt(size)

    def attend(head, block):
        start = pl.multiple_of(block * rows, rows)
        query = queries[head, pl.ds(start, rows), :]
        query_docs = doc_cols[pl.ds(start, rows), :]
        scores = []
        peak = None
        for step in range(2 * SPAN + 1):
            key = keys[head, pl.ds(start + step * rows, rows), :]
            key_docs = doc_rows[pl.ds(block + step, 1), :]
            raw = lax.dot_general(
                query, key, (((1,), (1,)), ((), ())), preferred_element_type=jnp.float32
            )
            masked = jnp.where(query_docs == key_docs, raw * scaling, MASKED)
            scores.append(masked)
            peak = masked if peak is None else jnp.maximum(peak, masked)
        peak = jnp.max(peak, axis=1, keepdims=True)
        totals = None
        summed = None
        for step in range(2 * SPAN + 1):
            value = values[head, pl.ds(start + step * rows, rows), :]
            weights = jnp.exp(scores[step] - peak)
            part = jnp.dot(
                weights.astype(jnp.bfloat16), value, preferred_element_type=jnp.float32
            )
            totals = weights if totals is None else totals + weights
            summed = part if summed is None else summed + part
        totals = jnp.sum(totals, axis=1, keepdims=True)
        results[head, pl.ds(start, rows), :] = (summed / totals).astype(jnp.bfloat16)

    def gather(head):
        for kind in ("key", "value"):
            own_copy(kind, head).wait()
            for offset in order:
                ring_arrival(kind, head, offset).wait_recv()
        for up in (True, False):
            for which in (0, 1):
                halo_copy(which, head, up).start()

    def compute(head):
        own_copy("query", head).wait()
        for offset in order:
            ring_arrival("query", head, offset).wait_recv()
        for up in (True, False):
            for which in (0, 1):
                halo_copy(which, head, up).wait_recv()

        @pl.loop(1, RING)
        def _(offset):
            target = ring_place(offset)
            attend(head, target)
            result_copy(head, target).start()

        attend(head, place)
        pltpu.make_async_copy(
            result_slot(head, place), out_ref.at[:, columns(place, head)], own_sem.at[head]
        ).start()

    gather(0)

    @pl.loop(0, own_heads - 1)
    def _(head):
        gather(head + 1)
        compute(head)

    compute(own_heads - 1)

    @pl.loop(0, own_heads)
    def _(head):
        pltpu.make_async_copy(
            result_slot(head, place), out_ref.at[:, columns(place, head)], own_sem.at[head]
        ).wait()
        for offset in order:
            result_arrival(head, ring_place(offset)).wait_recv()
            for kind in ("key", "value", "query"):
                ring_copy(kind, head, offset).wait_send()
            result_copy(head, ring_place(offset)).wait_send()
        for up in (True, False):
            for which in (0, 1):
                halo_copy(which, head, up).wait_send()


def on_device(query_states, key_states, value_states, doc_lengths):
    rows, width = query_states.shape
    outer_size = lax.axis_size("outer")
    inner_size = lax.axis_size("inner")
    size = width // HEADS
    own_heads = HEADS // RING
    window_rows = (RING + 2 * SPAN) * rows
    pair_sems = pltpu.SemaphoreType.DMA((own_heads, RING))
    hbm = pl.BlockSpec(memory_space=pl.ANY)
    return pl.pallas_call(
        functools.partial(kernel, outer_size, inner_size),
        out_shape=jax.ShapeDtypeStruct((rows, width), jnp.bfloat16),
        in_specs=[pl.BlockSpec(memory_space=pltpu.SMEM), hbm, hbm, hbm],
        out_specs=hbm,
        scratch_shapes=[
            pltpu.VMEM((own_heads, window_rows, size), jnp.bfloat16),
            pltpu.VMEM((own_heads, window_rows, size), jnp.bfloat16),
            pltpu.VMEM((own_heads, RING * rows, size), jnp.bfloat16),
            pltpu.VMEM((own_heads, RING * rows, size), jnp.bfloat16),
            pltpu.VMEM((16, rows), jnp.float32),
            pltpu.VMEM((RING * rows, rows), jnp.float32),
        ]
        + [pair_sems] * 8
        + [
            pltpu.SemaphoreType.DMA((own_heads, 2, 2)),
            pltpu.SemaphoreType.DMA((own_heads, 2, 2)),
            pltpu.SemaphoreType.DMA((own_heads,)),
        ],
        name="ring_heads_attention",
        compiler_params=pltpu.CompilerParams(
            collective_id=0, has_side_effects=True, vmem_limit_bytes=48 * 1024 * 1024
        ),
    )(doc_lengths, query_states, key_states, value_states)


def solution(mesh):
    return jax.shard_map(
        on_device,
        mesh=mesh,
        in_specs=(
            P(("outer", "inner"), None),
            P(("outer", "inner"), None),
            P(("outer", "inner"), None),
            P(),
        ),
        out_specs=P(("outer", "inner"), None),
        check_vma=False,
    )
```

```python
import functools
import math

import jax
import jax.numpy as jnp
from jax import lax
from jax.experimental import pallas as pl
from jax.experimental.pallas import tpu as pltpu
from jax.sharding import PartitionSpec as P

HEADS = 32
SPAN = 3
MESH = pl.DeviceIdType.MESH
MASKED = -1e30
LANES = 128
SUBLANES = 8


def pack_column(column):
    groups = column.shape[0] // SUBLANES
    shape = (SUBLANES, LANES)
    lane = lax.broadcasted_iota(jnp.int32, shape, 1)
    lane_in_group = lane % groups
    tile = jnp.broadcast_to(column[:SUBLANES], shape)
    for group in range(1, groups):
        part = column[group * SUBLANES : (group + 1) * SUBLANES]
        tile = jnp.where(lane_in_group == group, jnp.broadcast_to(part, shape), tile)
    folded = tile
    for pair in range(1, LANES // groups):
        shifted = pltpu.roll(tile, SUBLANES - 2 * pair, axis=0)
        folded = jnp.where(lane // groups == pair, shifted, folded)
    return folded[:2]


def unpack_column(packed, rows):
    groups = rows // SUBLANES
    shape = (SUBLANES, LANES)
    sublane = lax.broadcasted_iota(jnp.int32, shape, 0)
    stacked = jnp.concatenate([packed] * (SUBLANES // 2), axis=0)
    tile = stacked
    for pair in range(1, LANES // groups):
        shifted = pltpu.roll(stacked, LANES - groups * pair, axis=1)
        tile = jnp.where(sublane // 2 == pair, shifted, tile)
    return jnp.concatenate(
        [jnp.broadcast_to(tile[:, group : group + 1], shape) for group in range(groups)], axis=0
    )


def kernel(
    outer_size,
    inner_size,
    lengths_ref,
    query_ref,
    key_ref,
    value_ref,
    out_ref,
    queries,
    keys,
    values,
    results,
    in_data,
    in_stat,
    out_data,
    out_stat,
    bias,
    doc_rows,
    doc_cols,
    select,
    load_sem,
    store_sem,
    data_send,
    data_recv,
    stat_send,
    stat_recv,
):
    heads, rows, size = queries.shape
    slots = in_data.shape[2]
    doc_total = lengths_ref.shape[0]
    blocks = outer_size * inner_size
    outer = lax.axis_index("outer")
    inner = lax.axis_index("inner")
    block_index = outer * inner_size + inner
    scaling = 1.0 / math.sqrt(size)

    def device_of(block):
        wrapped = lax.rem(block + blocks, blocks)
        return (lax.div(wrapped, inner_size), lax.rem(wrapped, inner_size))

    neighbours = (device_of(block_index + 1), device_of(block_index - 1))

    barrier = pltpu.get_barrier_semaphore()
    for neighbour in neighbours:
        pl.semaphore_signal(barrier, inc=1, device_id=neighbour, device_id_type=MESH)

    def load(which, head):
        source = (query_ref, key_ref, value_ref)[which]
        target = (queries, keys, values)[which]
        columns = pl.ds(pl.multiple_of(head * size, size), size)
        return pltpu.make_async_copy(
            source.at[:, columns], target.at[head], load_sem.at[which, head]
        )

    def store(head):
        columns = pl.ds(pl.multiple_of(head * size, size), size)
        return pltpu.make_async_copy(
            results.at[head], out_ref.at[:, columns], store_sem.at[head]
        )

    @pl.loop(0, heads)
    def _(head):
        for which in range(3):
            load(which, head).start()

    positions = (
        (block_index - SPAN) * rows
        + lax.broadcasted_iota(jnp.int32, doc_rows.shape, 0) * rows
        + lax.broadcasted_iota(jnp.int32, doc_rows.shape, 1)
    )

    def count(doc, carry):
        end, counted = carry
        end = end + lengths_ref[doc]
        return end, counted + jnp.where(positions >= end, 1, 0)

    _, counted = lax.fori_loop(0, doc_total, count, (jnp.int32(0), jnp.zeros_like(positions)))
    inside = (positions >= 0) & (positions < blocks * rows)
    doc_rows[...] = jnp.where(inside, counted, -1).astype(jnp.float32)
    for block in range(2 * SPAN + 1):
        row = doc_rows[block : block + 1, :]
        column = jnp.transpose(jnp.broadcast_to(row, (LANES, rows)))
        doc_cols[block] = column
        for half in range(rows // LANES):
            lanes = slice(half * LANES, (half + 1) * LANES)
            key_docs = doc_rows[SPAN : SPAN + 1, lanes]
            bias[block, :, lanes] = jnp.where(column == key_docs, 0.0, MASKED)
    edges = (doc_rows[SPAN + 1 : SPAN + 2, 0:1], doc_rows[SPAN - 1 : SPAN, rows - 1 : rows])
    for way in range(2):
        sign = 1 - 2 * way
        for hop in range(SPAN):
            select[way, hop] = jnp.where(
                doc_cols[SPAN - sign * hop] == edges[way], 1.0, 0.0
            )

    pl.semaphore_wait(barrier, 2)

    def send(way, hop, slot):
        data = pltpu.make_async_remote_copy(
            src_ref=out_data.at[way, hop, slot],
            dst_ref=in_data.at[way, hop, slot],
            send_sem=data_send.at[way, hop, slot],
            recv_sem=data_recv.at[way, hop, slot],
            device_id=neighbours[way],
            device_id_type=MESH,
        )
        stat = pltpu.make_async_remote_copy(
            src_ref=out_stat.at[way, hop, slot, pl.ds(0, 2), :],
            dst_ref=in_stat.at[way, hop, slot, pl.ds(0, 2), :],
            send_sem=stat_send.at[way, hop, slot],
            recv_sem=stat_recv.at[way, hop, slot],
            device_id=neighbours[way],
            device_id_type=MESH,
        )
        return stat, data

    def arrive(way, hop, slot):
        for copy in send(way, hop, slot):
            copy.wait_recv()

    def attend(query, head, offset):
        raw = lax.dot_general(
            query, keys[head], (((1,), (1,)), ((), ())), preferred_element_type=jnp.float32
        )
        scores = raw * scaling + bias[SPAN + offset]
        peak = jnp.max(scores, axis=1, keepdims=True)
        weights = jnp.exp(scores - peak)
        total = jnp.sum(weights, axis=1, keepdims=True)
        summed = jnp.dot(
            weights.astype(jnp.bfloat16), values[head], preferred_element_type=jnp.float32
        )
        return summed, peak, total

    def arrived(way, hop, slot):
        data = in_data[way, hop, slot].astype(jnp.float32)
        return data, unpack_column(in_stat[way, hop, slot, 0:2, :], rows)[:, :1]

    def merge(partial, others):
        summed, peak, total = partial
        top = peak
        for _, level in others:
            top = jnp.maximum(top, level)
        own = jnp.exp(peak - top)
        summed = summed * own
        total = total * own
        for data, level in others:
            share = jnp.exp(level - top)
            summed = summed + data * share
            total = total + share
        return summed / total, top + jnp.log(total)

    def put(way, hop, slot, query, output, level):
        taken = select[way, hop] > 0.5
        out_data[way, hop, slot] = jnp.where(
            taken, query.astype(jnp.float32), output
        ).astype(jnp.bfloat16)
        out_stat[way, hop, slot, 0:2, :] = pack_column(
            jnp.where(taken[:, :1], MASKED, level)
        )
        for copy in send(way, hop, slot):
            copy.start()

    def pass_on(step, hop):
        slot = step - hop
        for way in range(2):
            sign = 1 - 2 * way
            if hop == 0:
                query = queries[jnp.minimum(step, heads - 1)]
            else:
                query = in_data[way, hop - 1, slot]
            head = step - SPAN - 1 - hop

            @pl.when(head >= 0)
            def _():
                back = in_data[1 - way, SPAN - 1 - hop, head]
                partial = attend(back, head, sign * (SPAN - hop))
                others = [arrived(way, hop - 1, slot)] if hop else []
                output, level = merge(partial, others)
                put(way, hop, slot, query, output, level)

            @pl.when(head < 0)
            def _():
                put(
                    way,
                    hop,
                    slot,
                    query,
                    jnp.zeros((rows, size), jnp.float32),
                    jnp.full((rows, 1), MASKED, jnp.float32),
                )

    last = slots + SPAN

    @pl.loop(0, last + 1)
    def _(step):
        @pl.when(step < heads)
        def _():
            load(0, step).wait()

        @pl.when((step >= SPAN + 1) & (step < SPAN + 1 + heads))
        def _():
            for which in (1, 2):
                load(which, step - SPAN - 1).wait()

        @pl.when(step >= SPAN + 1)
        def _():
            for way in range(2):
                arrive(way, SPAN - 1, step - SPAN - 1)

        for hop in range(SPAN):

            @pl.when((step >= hop) & (step < slots + hop))
            def _():
                if hop:
                    for way in range(2):
                        arrive(way, hop - 1, step - hop)
                pass_on(step, hop)

        @pl.when(step >= 2 * SPAN + 2)
        def _():
            head = step - 2 * SPAN - 2
            partial = attend(queries[head], head, 0)
            others = [arrived(way, SPAN - 1, step - SPAN - 1) for way in range(2)]
            output, _ = merge(partial, others)
            results[head] = output.astype(jnp.bfloat16)
            store(head).start()

    @pl.loop(0, heads)
    def _(head):
        store(head).wait()

    @pl.loop(0, slots)
    def _(slot):
        for way in range(2):
            for hop in range(SPAN):
                for copy in send(way, hop, slot):
                    copy.wait_send()


def on_device(query_states, key_states, value_states, doc_lengths):
    rows, width = query_states.shape
    size = width // HEADS
    slots = HEADS + SPAN + 1
    hbm = pl.BlockSpec(memory_space=pl.ANY)
    mail = pltpu.VMEM((2, SPAN, slots, rows, size), jnp.bfloat16)
    stats = pltpu.VMEM((2, SPAN, slots, SUBLANES, LANES), jnp.float32)
    held = pltpu.VMEM((HEADS, rows, size), jnp.bfloat16)
    mail_sems = pltpu.SemaphoreType.DMA((2, SPAN, slots))
    return pl.pallas_call(
        functools.partial(kernel, lax.axis_size("outer"), lax.axis_size("inner")),
        out_shape=jax.ShapeDtypeStruct((rows, width), jnp.bfloat16),
        in_specs=[pl.BlockSpec(memory_space=pltpu.SMEM), hbm, hbm, hbm],
        out_specs=hbm,
        scratch_shapes=[
            held,
            held,
            held,
            held,
            mail,
            stats,
            mail,
            stats,
            pltpu.VMEM((2 * SPAN + 1, rows, rows), jnp.float32),
            pltpu.VMEM((SUBLANES, rows), jnp.float32),
            pltpu.VMEM((2 * SPAN + 1, rows, LANES), jnp.float32),
            pltpu.VMEM((2, SPAN, rows, LANES), jnp.float32),
            pltpu.SemaphoreType.DMA((3, HEADS)),
            pltpu.SemaphoreType.DMA((HEADS,)),
            mail_sems,
            mail_sems,
            mail_sems,
            mail_sems,
        ],
        name="query_mail_attention",
        compiler_params=pltpu.CompilerParams(
            collective_id=0, has_side_effects=True, vmem_limit_bytes=56 * 1024 * 1024
        ),
    )(doc_lengths, query_states, key_states, value_states)


def solution(mesh):
    return jax.shard_map(
        on_device,
        mesh=mesh,
        in_specs=(
            P(("outer", "inner"), None),
            P(("outer", "inner"), None),
            P(("outer", "inner"), None),
            P(),
        ),
        out_specs=P(("outer", "inner"), None),
        check_vma=False,
    )
```

```python
import functools
import math

import jax
import jax.numpy as jnp
from jax import lax
from jax.experimental import pallas as pl
from jax.experimental.pallas import tpu as pltpu
from jax.sharding import PartitionSpec as P

HEADS = 32
SPAN = 3
MESH = pl.DeviceIdType.MESH
MASKED = -1e30
LANES = 128
SUBLANES = 8


def flip(block):
    return jnp.transpose(block.astype(jnp.float32)).astype(jnp.bfloat16)


def kernel(
    outer_size,
    inner_size,
    lengths_ref,
    query_ref,
    key_ref,
    value_ref,
    out_ref,
    queries,
    keys,
    values,
    results,
    in_data,
    in_stat,
    out_data,
    out_stat,
    bias,
    doc_rows,
    select,
    queries_t,
    values_t,
    load_sem,
    store_sem,
    data_send,
    data_recv,
    stat_send,
    stat_recv,
):
    heads, rows, size = queries.shape
    slots = in_data.shape[2]
    doc_total = lengths_ref.shape[0]
    blocks = outer_size * inner_size
    outer = lax.axis_index("outer")
    inner = lax.axis_index("inner")
    block_index = outer * inner_size + inner
    scaling = 1.0 / math.sqrt(size)

    def device_of(block):
        wrapped = lax.rem(block + blocks, blocks)
        return (lax.div(wrapped, inner_size), lax.rem(wrapped, inner_size))

    neighbours = (device_of(block_index + 1), device_of(block_index - 1))

    barrier = pltpu.get_barrier_semaphore()
    for neighbour in neighbours:
        pl.semaphore_signal(barrier, inc=1, device_id=neighbour, device_id_type=MESH)

    def load(which, head):
        source = (query_ref, key_ref, value_ref)[which]
        target = (queries, keys, values)[which]
        columns = pl.ds(pl.multiple_of(head * size, size), size)
        return pltpu.make_async_copy(
            source.at[:, columns], target.at[head], load_sem.at[which, head]
        )

    def store(head):
        columns = pl.ds(pl.multiple_of(head * size, size), size)
        return pltpu.make_async_copy(
            results.at[head], out_ref.at[:, columns], store_sem.at[head]
        )

    @pl.loop(0, heads)
    def _(head):
        for which in range(3):
            load(which, head).start()

    positions = (
        (block_index - SPAN) * rows
        + lax.broadcasted_iota(jnp.int32, doc_rows.shape, 0) * rows
        + lax.broadcasted_iota(jnp.int32, doc_rows.shape, 1)
    )

    def count(doc, carry):
        end, counted = carry
        end = end + lengths_ref[doc]
        return end, counted + jnp.where(positions >= end, 1, 0)

    _, counted = lax.fori_loop(0, doc_total, count, (jnp.int32(0), jnp.zeros_like(positions)))
    inside = (positions >= 0) & (positions < blocks * rows)
    doc_rows[...] = jnp.where(inside, counted, -1).astype(jnp.float32)
    own_docs = jnp.transpose(jnp.broadcast_to(doc_rows[SPAN : SPAN + 1, :], (LANES, rows)))
    for block in range(2 * SPAN + 1):
        for half in range(rows // LANES):
            lanes = slice(half * LANES, (half + 1) * LANES)
            bias[block, :, lanes] = jnp.where(
                own_docs == doc_rows[block : block + 1, lanes], 0.0, MASKED
            )
    edges = (doc_rows[SPAN + 1 : SPAN + 2, 0:1], doc_rows[SPAN - 1 : SPAN, rows - 1 : rows])
    for way in range(2):
        sign = 1 - 2 * way
        for hop in range(SPAN):
            block = SPAN - sign * hop
            select[way, hop] = jnp.where(doc_rows[block : block + 1, :] == edges[way], 1.0, 0.0)

    pl.semaphore_wait(barrier, 2)

    def send(way, hop, slot):
        data = pltpu.make_async_remote_copy(
            src_ref=out_data.at[way, hop, slot],
            dst_ref=in_data.at[way, hop, slot],
            send_sem=data_send.at[way, hop, slot],
            recv_sem=data_recv.at[way, hop, slot],
            device_id=neighbours[way],
            device_id_type=MESH,
        )
        stat = pltpu.make_async_remote_copy(
            src_ref=out_stat.at[way, hop, slot],
            dst_ref=in_stat.at[way, hop, slot],
            send_sem=stat_send.at[way, hop, slot],
            recv_sem=stat_recv.at[way, hop, slot],
            device_id=neighbours[way],
            device_id_type=MESH,
        )
        return stat, data

    def arrive(way, hop, slot):
        for copy in send(way, hop, slot):
            copy.wait_recv()

    def attend(query, head, offset):
        raw = jnp.dot(keys[head], query, preferred_element_type=jnp.float32)
        scores = raw * scaling + bias[SPAN + offset]
        peak = jnp.max(scores, axis=0, keepdims=True)
        weights = jnp.exp(scores - peak)
        total = jnp.sum(weights, axis=0, keepdims=True)
        summed = jnp.dot(
            values_t[head], weights.astype(jnp.bfloat16), preferred_element_type=jnp.float32
        )
        return summed, peak, total

    def arrived(way, hop, slot):
        return in_data[way, hop, slot].astype(jnp.float32), in_stat[way, hop, slot]

    def merge(partial, others):
        summed, peak, total = partial
        top = peak
        for _, level in others:
            top = jnp.maximum(top, level)
        own = jnp.exp(peak - top)
        total = total * own
        shares = [jnp.exp(level - top) for _, level in others]
        for share in shares:
            total = total + share
        inverse = 1.0 / total
        summed = summed * (own * inverse)
        for (data, _), share in zip(others, shares):
            summed = summed + data * (share * inverse)
        return summed, top + jnp.log(total)

    def put(way, hop, slot, query, output, level):
        taken = select[way, hop]
        out_data[way, hop, slot] = jnp.where(
            jnp.broadcast_to(taken, (size, rows)) > 0.5, query.astype(jnp.float32), output
        ).astype(jnp.bfloat16)
        out_stat[way, hop, slot] = jnp.where(taken > 0.5, MASKED, level)

    def post(hop, slot):
        for way in range(2):
            for copy in send(way, hop, slot):
                copy.start()

    def query_of(way, hop, step):
        if hop == 0:
            return queries_t[jnp.minimum(step, heads - 1)]
        return in_data[way, hop - 1, step - hop]

    def pass_on(step, hop, steady):
        slot = step - hop
        head = step - SPAN - 1 - hop

        def partials():
            return [
                attend(
                    in_data[1 - way, SPAN - 1 - hop, head], head, (1 - 2 * way) * (SPAN - hop)
                )
                for way in range(2)
            ]

        def arrivals():
            if hop:
                for way in range(2):
                    arrive(way, hop - 1, slot)

        def outputs(parts):
            for way in range(2):
                others = [arrived(way, hop - 1, slot)] if hop else []
                output, level = merge(parts[way], others)
                put(way, hop, slot, query_of(way, hop, step), output, level)
            post(hop, slot)

        if steady:
            parts = partials()
            arrivals()
            outputs(parts)
            return

        arrivals()

        @pl.when(head >= 0)
        def _():
            outputs(partials())

        @pl.when(head < 0)
        def _():
            for way in range(2):
                put(
                    way,
                    hop,
                    slot,
                    query_of(way, hop, step),
                    jnp.zeros((size, rows), jnp.float32),
                    jnp.full((1, rows), MASKED, jnp.float32),
                )
            post(hop, slot)

    last = slots + SPAN

    def advance(step, steady):
        def guard(condition):
            return (lambda body: body()) if steady else pl.when(condition)

        @guard(step < heads)
        def _():
            load(0, step).wait()
            queries_t[step] = flip(queries[step])

        @guard((step >= SPAN + 1) & (step < SPAN + 1 + heads))
        def _():
            head = step - SPAN - 1
            for which in (1, 2):
                load(which, head).wait()
            values_t[head] = flip(values[head])

        @guard(step >= SPAN + 1)
        def _():
            for way in range(2):
                arrive(way, SPAN - 1, step - SPAN - 1)

        for hop in range(SPAN):

            @guard((step >= hop) & (step < slots + hop))
            def _(hop=hop):
                pass_on(step, hop, steady)

        @guard(step >= 2 * SPAN + 2)
        def _():
            head = step - 2 * SPAN - 2
            partial = attend(queries_t[head], head, 0)
            others = [arrived(way, SPAN - 1, step - SPAN - 1) for way in range(2)]
            output, _ = merge(partial, others)
            results[head] = jnp.transpose(output).astype(jnp.bfloat16)
            store(head).start()

    first = 2 * SPAN + 2

    @pl.loop(0, first)
    def _(step):
        advance(step, False)

    @pl.loop(first, heads)
    def _(step):
        advance(step, True)

    @pl.loop(heads, last + 1)
    def _(step):
        advance(step, False)

    @pl.loop(0, heads)
    def _(head):
        store(head).wait()

    @pl.loop(0, slots)
    def _(slot):
        for way in range(2):
            for hop in range(SPAN):
                for copy in send(way, hop, slot):
                    copy.wait_send()


def on_device(query_states, key_states, value_states, doc_lengths):
    rows, width = query_states.shape
    size = width // HEADS
    slots = HEADS + SPAN + 1
    hbm = pl.BlockSpec(memory_space=pl.ANY)
    mail = pltpu.VMEM((2, SPAN, slots, size, rows), jnp.bfloat16)
    stats = pltpu.VMEM((2, SPAN, slots, 1, rows), jnp.float32)
    held = pltpu.VMEM((HEADS, rows, size), jnp.bfloat16)
    held_t = pltpu.VMEM((HEADS, size, rows), jnp.bfloat16)
    mail_sems = pltpu.SemaphoreType.DMA((2, SPAN, slots))
    return pl.pallas_call(
        functools.partial(kernel, lax.axis_size("outer"), lax.axis_size("inner")),
        out_shape=jax.ShapeDtypeStruct((rows, width), jnp.bfloat16),
        in_specs=[pl.BlockSpec(memory_space=pltpu.SMEM), hbm, hbm, hbm],
        out_specs=hbm,
        scratch_shapes=[
            held,
            held,
            held,
            held,
            mail,
            stats,
            mail,
            stats,
            pltpu.VMEM((2 * SPAN + 1, rows, rows), jnp.float32),
            pltpu.VMEM((SUBLANES, rows), jnp.float32),
            pltpu.VMEM((2, SPAN, 1, rows), jnp.float32),
            held_t,
            held_t,
            pltpu.SemaphoreType.DMA((3, HEADS)),
            pltpu.SemaphoreType.DMA((HEADS,)),
            mail_sems,
            mail_sems,
            mail_sems,
            mail_sems,
        ],
        name="query_mail_attention",
        compiler_params=pltpu.CompilerParams(
            collective_id=0, has_side_effects=True, vmem_limit_bytes=56 * 1024 * 1024
        ),
    )(doc_lengths, query_states, key_states, value_states)


def solution(mesh):
    return jax.shard_map(
        on_device,
        mesh=mesh,
        in_specs=(
            P(("outer", "inner"), None),
            P(("outer", "inner"), None),
            P(("outer", "inner"), None),
            P(),
        ),
        out_specs=P(("outer", "inner"), None),
        check_vma=False,
    )
```

```python
import functools
import math

import jax
import jax.numpy as jnp
from jax import lax
from jax.experimental import pallas as pl
from jax.experimental.pallas import tpu as pltpu
from jax.sharding import PartitionSpec as P

HEADS = 32
SPAN = 3
RING = 8
MESH = pl.DeviceIdType.MESH
MASKED = -1e30


def kernel(
    outer_size,
    inner_size,
    lengths_ref,
    query_ref,
    key_ref,
    value_ref,
    out_ref,
    keys,
    values,
    queries,
    results,
    doc_rows,
    doc_cols,
    key_send,
    key_recv,
    value_send,
    value_recv,
    query_send,
    query_recv,
    result_send,
    result_recv,
    halo_send,
    halo_recv,
    own_sem,
):
    rows = query_ref.shape[0]
    size = keys.shape[2]
    own_heads = keys.shape[0]
    group_cols = own_heads * size
    halo_rows = SPAN * rows
    doc_total = lengths_ref.shape[0]
    blocks = outer_size * inner_size
    outer = lax.axis_index("outer")
    inner = lax.axis_index("inner")
    place = lax.rem(inner, RING)
    line_start = inner - place
    block_index = outer * inner_size + inner

    def ring_device(other):
        return (outer, line_start + other)

    def group_device(step):
        other = lax.rem(block_index + step * RING + blocks, blocks)
        return (lax.div(other, inner_size), lax.rem(other, inner_size))

    def ring_place(offset):
        return lax.rem(place + offset, RING)

    def columns(owner, head):
        return pl.ds(pl.multiple_of(owner * group_cols + head * size, size), size)

    def key_slot(head, source):
        return keys.at[head, pl.ds(pl.multiple_of(halo_rows + source * rows, rows), rows), :]

    def value_slot(head, source):
        return values.at[head, pl.ds(pl.multiple_of(halo_rows + source * rows, rows), rows), :]

    def query_slot(head, source):
        return queries.at[head, pl.ds(pl.multiple_of(source * rows, rows), rows), :]

    def result_slot(head, target):
        return results.at[head, pl.ds(pl.multiple_of(target * rows, rows), rows), :]

    streams = {
        "key": (key_ref, key_slot, key_send, key_recv),
        "value": (value_ref, value_slot, value_send, value_recv),
        "query": (query_ref, query_slot, query_send, query_recv),
    }

    def ring_copy(kind, head, offset):
        source, slot, send, recv = streams[kind]
        owner = ring_place(offset)
        return pltpu.make_async_remote_copy(
            src_ref=source.at[:, columns(owner, head)],
            dst_ref=slot(head, place),
            send_sem=send.at[head, owner],
            recv_sem=recv.at[head, place],
            device_id=ring_device(owner),
            device_id_type=MESH,
        )

    def ring_arrival(kind, head, offset):
        source, slot, send, recv = streams[kind]
        other = ring_place(offset)
        return pltpu.make_async_remote_copy(
            src_ref=source.at[:, columns(other, head)],
            dst_ref=slot(head, other),
            send_sem=send.at[head, other],
            recv_sem=recv.at[head, other],
            device_id=ring_device(other),
            device_id_type=MESH,
        )

    def own_copy(kind, head):
        source, slot, send, recv = streams[kind]
        return pltpu.make_async_copy(
            source.at[:, columns(place, head)], slot(head, place), recv.at[head, place]
        )

    def halo_copy(which, head, up):
        buffer = (keys, values)[which]
        edge = halo_rows + RING * rows
        source_row = edge - halo_rows if up else halo_rows
        target_row = 0 if up else edge
        return pltpu.make_async_remote_copy(
            src_ref=buffer.at[head, pl.ds(source_row, halo_rows), :],
            dst_ref=buffer.at[head, pl.ds(target_row, halo_rows), :],
            send_sem=halo_send.at[head, which, 0 if up else 1],
            recv_sem=halo_recv.at[head, which, 0 if up else 1],
            device_id=group_device(1 if up else -1),
            device_id_type=MESH,
        )

    def result_copy(head, target):
        return pltpu.make_async_remote_copy(
            src_ref=result_slot(head, target),
            dst_ref=out_ref.at[:, columns(place, head)],
            send_sem=result_send.at[head, target],
            recv_sem=result_recv.at[head, place],
            device_id=ring_device(target),
            device_id_type=MESH,
        )

    def result_arrival(head, source):
        return pltpu.make_async_remote_copy(
            src_ref=result_slot(head, source),
            dst_ref=out_ref.at[:, columns(source, head)],
            send_sem=result_send.at[head, source],
            recv_sem=result_recv.at[head, source],
            device_id=ring_device(source),
            device_id_type=MESH,
        )

    barrier = pltpu.get_barrier_semaphore()
    for offset in range(1, RING):
        pl.semaphore_signal(
            barrier, inc=1, device_id=ring_device(ring_place(offset)), device_id_type=MESH
        )
    for step in (1, -1):
        pl.semaphore_signal(
            barrier, inc=1, device_id=group_device(step), device_id_type=MESH
        )
    pl.semaphore_wait(barrier, RING + 1)

    order = (1, 7, 2, 6, 3, 5, 4)

    @pl.loop(0, own_heads)
    def _(head):
        for kind in ("key", "value", "query"):
            own_copy(kind, head).start()
            for offset in order:
                ring_copy(kind, head, offset).start()

    window = 2 * SPAN + RING
    first_position = (block_index - place - SPAN) * rows
    positions = (
        first_position
        + lax.broadcasted_iota(jnp.int32, doc_rows.shape, 0) * rows
        + lax.broadcasted_iota(jnp.int32, doc_rows.shape, 1)
    )

    def count(doc, carry):
        end, counted = carry
        end = end + lengths_ref[doc]
        return end, counted + jnp.where(positions >= end, 1, 0)

    _, counted = lax.fori_loop(0, doc_total, count, (jnp.int32(0), jnp.zeros_like(positions)))
    inside = (positions >= 0) & (positions < blocks * rows)
    doc_rows[...] = jnp.where(inside, counted, -1).astype(jnp.float32)
    for block in range(RING):
        row = doc_rows[SPAN + block : SPAN + block + 1, :]
        doc_cols[block * rows : (block + 1) * rows, :] = jnp.transpose(
            jnp.broadcast_to(row, (rows, rows))
        )

    scaling = 1.0 / math.sqrt(size)

    def attend(head, block):
        start = pl.multiple_of(block * rows, rows)
        query = queries[head, pl.ds(start, rows), :]
        query_docs = doc_cols[pl.ds(start, rows), :]
        scores = []
        peak = None
        for step in range(2 * SPAN + 1):
            key = keys[head, pl.ds(start + step * rows, rows), :]
            key_docs = doc_rows[pl.ds(block + step, 1), :]
            raw = lax.dot_general(
                query, key, (((1,), (1,)), ((), ())), preferred_element_type=jnp.float32
            )
            masked = jnp.where(query_docs == key_docs, raw * scaling, MASKED)
            scores.append(masked)
            peak = masked if peak is None else jnp.maximum(peak, masked)
        peak = jnp.max(peak, axis=1, keepdims=True)
        totals = None
        summed = None
        for step in range(2 * SPAN + 1):
            value = values[head, pl.ds(start + step * rows, rows), :]
            weights = jnp.exp(scores[step] - peak)
            part = jnp.dot(
                weights.astype(jnp.bfloat16), value, preferred_element_type=jnp.float32
            )
            totals = weights if totals is None else totals + weights
            summed = part if summed is None else summed + part
        totals = jnp.sum(totals, axis=1, keepdims=True)
        results[head, pl.ds(start, rows), :] = (summed / totals).astype(jnp.bfloat16)

    def gather(head):
        for kind in ("key", "value"):
            own_copy(kind, head).wait()
            for offset in order:
                ring_arrival(kind, head, offset).wait_recv()
        for up in (True, False):
            for which in (0, 1):
                halo_copy(which, head, up).start()

    def compute(head):
        own_copy("query", head).wait()
        for offset in order:
            ring_arrival("query", head, offset).wait_recv()
        for up in (True, False):
            for which in (0, 1):
                halo_copy(which, head, up).wait_recv()

        @pl.loop(0, RING - 1)
        def _(turn):
            half = lax.div(turn + 1, 2)
            target = ring_place(RING // 2 + half * (1 - 2 * lax.rem(turn, 2)))
            attend(head, target)
            result_copy(head, target).start()

        attend(head, place)
        pltpu.make_async_copy(
            result_slot(head, place), out_ref.at[:, columns(place, head)], own_sem.at[head]
        ).start()

    gather(0)

    @pl.loop(0, own_heads - 1)
    def _(head):
        gather(head + 1)
        compute(head)

    compute(own_heads - 1)

    @pl.loop(0, own_heads)
    def _(head):
        pltpu.make_async_copy(
            result_slot(head, place), out_ref.at[:, columns(place, head)], own_sem.at[head]
        ).wait()
        for offset in order:
            result_arrival(head, ring_place(offset)).wait_recv()
            for kind in ("key", "value", "query"):
                ring_copy(kind, head, offset).wait_send()
            result_copy(head, ring_place(offset)).wait_send()
        for up in (True, False):
            for which in (0, 1):
                halo_copy(which, head, up).wait_send()


def on_device(query_states, key_states, value_states, doc_lengths):
    rows, width = query_states.shape
    outer_size = lax.axis_size("outer")
    inner_size = lax.axis_size("inner")
    size = width // HEADS
    own_heads = HEADS // RING
    window_rows = (RING + 2 * SPAN) * rows
    pair_sems = pltpu.SemaphoreType.DMA((own_heads, RING))
    hbm = pl.BlockSpec(memory_space=pl.ANY)
    return pl.pallas_call(
        functools.partial(kernel, outer_size, inner_size),
        out_shape=jax.ShapeDtypeStruct((rows, width), jnp.bfloat16),
        in_specs=[pl.BlockSpec(memory_space=pltpu.SMEM), hbm, hbm, hbm],
        out_specs=hbm,
        scratch_shapes=[
            pltpu.VMEM((own_heads, window_rows, size), jnp.bfloat16),
            pltpu.VMEM((own_heads, window_rows, size), jnp.bfloat16),
            pltpu.VMEM((own_heads, RING * rows, size), jnp.bfloat16),
            pltpu.VMEM((own_heads, RING * rows, size), jnp.bfloat16),
            pltpu.VMEM((16, rows), jnp.float32),
            pltpu.VMEM((RING * rows, rows), jnp.float32),
        ]
        + [pair_sems] * 8
        + [
            pltpu.SemaphoreType.DMA((own_heads, 2, 2)),
            pltpu.SemaphoreType.DMA((own_heads, 2, 2)),
            pltpu.SemaphoreType.DMA((own_heads,)),
        ],
        name="ring_heads_attention",
        compiler_params=pltpu.CompilerParams(
            collective_id=0, has_side_effects=True, vmem_limit_bytes=48 * 1024 * 1024
        ),
    )(doc_lengths, query_states, key_states, value_states)


def solution(mesh):
    return jax.shard_map(
        on_device,
        mesh=mesh,
        in_specs=(
            P(("outer", "inner"), None),
            P(("outer", "inner"), None),
            P(("outer", "inner"), None),
            P(),
        ),
        out_specs=P(("outer", "inner"), None),
        check_vma=False,
    )
```
